256 devices in a mesh: seq: 32 (over z, y), exp: 4 (over x), dp: 2 (over core).
Axes of the slice: x: 4, y: 4, z: 8, core: 2. Of those that a mesh axis runs over, the one named last changes fastest.
Arguments:
- head_inputs: bfloat16 [16384, 4096], P(('dp', 'seq'), 'exp'), parts along dimension 0, may hold values from -6 to 6
- input_matrix: bfloat16 [16384, 128], P(('dp', 'seq')), parts along dimension 0, may hold values from -0.015625 to 0.015625
- output_matrix: bfloat16 [16384, 128], P(('dp', 'seq')), parts along dimension 0, may hold values from -6 to 6
- log_decay: float32 [64, 16384], P('exp', ('dp', 'seq')), parts along dimension 1, may hold values from -1 to 0
- skip_gain: float32 [64], P('exp'), may hold values from 0.5 to 1.5
- residual: bfloat16 [16384, 4096], P(('dp', 'seq', 'exp')), parts along dimension 0, may hold values from -6 to 6
- norm_gain: float32 [4096], replicated, may hold values from 0.1 to 1.9
- router_weight: bfloat16 [4096, 16], replicated, may hold values from -0.09375 to 0.09375
- expert_ids: int32 [16384, 2], P(('dp', 'seq', 'exp')), parts along dimension 0, may hold values from 0 to 15, as said below
- gate_weight: bfloat16 [4, 4096, 12288], P('exp', None, 'seq'), may hold values from -0.09375 to 0.09375
- up_weight: bfloat16 [4, 4096, 12288], P('exp', None, 'seq'), may hold values from -0.09375 to 0.09375
- down_weight: bfloat16 [4, 12288, 4096], P('exp', 'seq'), may hold values from -0.0546875 to 0.0546875
Outputs:
- layer_out: bfloat16 [16384, 4096], P(('dp', 'seq', 'exp')), parts along dimension 0
The draws below stay inside these ranges and needn't reach their ends.
There are 2 independent parts, one for each index of `dp`. The reference program is written for one: setup_inputs(seed, part) draws one part's arguments, and reference() takes and returns one part's arrays. A program takes and returns all parts, laid end to end along the dimension named above; an argument that names none is the same for every part. Nothing has to cross between parts.
Inputs may be any that keep to these rules, and one draw needn't show every extreme that they name: `expert_ids`: each row names two different experts; the second column never names an expert below 4. In every aligned block of 64 rows each expert below 4 is named by at most 8 rows, and in every run of 4 consecutive blocks, starting at block 0, by at most 16 rows; in every run one such expert is named by exactly 8 rows in one block and by exactly 16 rows in the whole run.
All inputs are finite; a program needn't handle non-finite values.
Results may differ from the reference program's by a relative error of at most 0.015.
Values may be sent and summed in bfloat16 or wider, within the bound.
A program may use at most 128 MiB of HBM per device.

```python
import math
import jax
import jax.numpy as jnp
from jax import lax

D = 4096
RECURRENT_PARTS = 64
P_SIZE = 64
N = 128
EXPERTS = 16
FFW = 12288
TOK_DEV = 256
STRING_ELEMENTS = 8192
ROWS = 64
CAP = 8
FLIGHT = 4
N_SEQ = 32


def draw_log_decay(key, part):
    prng_seeds = jax.random.split(jax.random.fold_in(key, 11), 7)
    threshold = 5
    slow = jax.random.randint(prng_seeds[0], (RECURRENT_PARTS,), 0, 10) < threshold
    slow_rate = jnp.exp(jax.random.uniform(prng_seeds[1], (RECURRENT_PARTS,), jnp.float32, math.log(0.05), math.log(0.5))) / STRING_ELEMENTS
    fast_rate = 1.0 / jnp.exp(jax.random.uniform(prng_seeds[2], (RECURRENT_PARTS,), jnp.float32, math.log(30.0), math.log(50.0)))
    rate = jnp.where(slow, slow_rate, fast_rate)
    token_factor = jax.random.uniform(prng_seeds[3], (RECURRENT_PARTS, STRING_ELEMENTS), jnp.float32, 0.5, 1.5)
    segments = (STRING_ELEMENTS + 127) // 128
    segment_factor = jnp.exp(jax.random.uniform(prng_seeds[4], (RECURRENT_PARTS, segments), jnp.float32, math.log(0.5), math.log(2.0)))
    segment_wide = jnp.repeat(segment_factor, 128, axis=1)[:, :STRING_ELEMENTS]
    default_entry = -rate[:, None] * token_factor * segment_wide
    spike_indices = jax.random.randint(prng_seeds[5], (2,), 0, STRING_ELEMENTS)
    element_indices = jnp.arange(STRING_ELEMENTS)
    spike_enabled = jnp.any(element_indices[None, :] == spike_indices[:, None], axis=0)
    spike_extent = jax.random.uniform(prng_seeds[6], (RECURRENT_PARTS,), jnp.float32, math.log(0.5), math.log(0.8))
    return (default_entry + jnp.where(spike_enabled[None, :], spike_extent[:, None], 0.0)).astype(jnp.float32)


def draw_expert_ids(key, part):
    prng_seeds = jax.random.split(jax.random.fold_in(key, 23), 8)
    blocks = STRING_ELEMENTS // ROWS
    runs = blocks // FLIGHT
    block_iota = jnp.arange(blocks)
    run_of = block_iota // FLIGHT
    within_run = block_iota % FLIGHT
    hottest_run = jax.random.randint(prng_seeds[0], (runs,), 0, FLIGHT)
    full_block = jax.random.randint(prng_seeds[6], (runs,), 0, FLIGHT)
    unit_pick = jax.random.randint(prng_seeds[7], (runs, CAP), 0, FLIGHT - 1)
    unit_block = unit_pick + (unit_pick >= full_block[:, None]).astype(jnp.int32)
    flight_iota = jnp.arange(FLIGHT)
    unit_counts = jnp.sum((unit_block[:, :, None] == flight_iota[None, None, :]).astype(jnp.int32), axis=1)
    hot_counts = jnp.where(flight_iota[None, :] == full_block[:, None], CAP, unit_counts)
    hot_here = jnp.sum(jnp.where(within_run[:, None] == flight_iota[None, :], hot_counts[run_of], 0), axis=1)
    hottest = hottest_run[run_of]
    others = jax.random.randint(prng_seeds[1], (blocks, FLIGHT), CAP // 4, CAP // 2 + 1)
    counts = jnp.where(flight_iota[None, :] == hottest[:, None], hot_here[:, None], others)
    ends = jnp.cumsum(counts, axis=1)
    starts = ends - counts
    places = jnp.arange(ROWS)
    inside = (places[None, None, :] >= starts[:, :, None]) & (places[None, None, :] < ends[:, :, None])
    labels = jnp.sum(jnp.where(inside, flight_iota[None, :, None] + 1, 0), axis=1) - 1
    scores = jax.random.randint(prng_seeds[2], (blocks, ROWS), 0, 1 << 20) * ROWS + places[None, :]
    order = jnp.argsort(scores, axis=1)
    shuffled = jnp.take_along_axis(labels, order, axis=1)
    spare = EXPERTS - FLIGHT
    filler = jax.random.randint(prng_seeds[3], (blocks, ROWS), 0, spare) + FLIGHT
    first = jnp.where(shuffled >= 0, shuffled, filler)
    offsets = jax.random.randint(prng_seeds[4], (blocks, ROWS), 1, spare)
    fresh = jax.random.randint(prng_seeds[5], (blocks, ROWS), 0, spare) + FLIGHT
    second = jnp.where(first >= FLIGHT, FLIGHT + (first - FLIGHT + offsets) % spare, fresh)
    return jnp.stack([first, second], axis=-1).reshape(STRING_ELEMENTS, 2).astype(jnp.int32)


def levels(stream_key, shape, pieces, low, top_value):
    level, own = 1.0, jax.random.fold_in(stream_key, 6)
    for axis_at, parts in pieces:
        steps = jnp.exp(jax.random.uniform(jax.random.fold_in(own, axis_at), (parts,), jnp.float32, low / len(pieces), top_value / len(pieces)))
        level = level * jnp.repeat(steps, shape[axis_at] // parts).reshape([-1 if axis == axis_at else 1 for axis in range(len(shape))])
    return level


def centred(stream_key, dims, deviation, reach, cuts=(), dtype=jnp.bfloat16):
    array = jax.random.normal(stream_key, dims, jnp.float32) * deviation
    if len(cuts) > 0:
        array = levels(stream_key, dims, cuts, -0.22, 0.18) * array
    return jnp.clip(array, min=-reach, max=reach).astype(dtype)


def setup_inputs(seed: int = 0, part: int = 0) -> dict:
    key_of = jax.random.split(jax.random.key(seed), 13)
    part_keys = jax.random.split(jax.random.fold_in(key_of[12], part), 13)
    return {
        "head_inputs": centred(part_keys[0], (STRING_ELEMENTS, RECURRENT_PARTS * P_SIZE), 1.0, 6.0, ((0, 32), (1, 4))),
        "input_matrix": centred(part_keys[1], (STRING_ELEMENTS, N), ((N * STRING_ELEMENTS) ** -0.5), 0.015625, ((0, 32),)),
        "output_matrix": centred(part_keys[2], (STRING_ELEMENTS, N), 1.0, 6.0, ((0, 32),)),
        "log_decay": draw_log_decay(jax.random.fold_in(jax.random.fold_in(key_of[12], part), 71), part),
        "skip_gain": jnp.clip(0.5 + 1.0 * jax.random.uniform(key_of[4], (RECURRENT_PARTS,), jnp.float32) ** levels(key_of[4], (RECURRENT_PARTS,), ((0, 4),), -0.2, 0.2), 0.5, 1.5),
        "residual": centred(part_keys[5], (STRING_ELEMENTS, D), 1.0, 6.0, ((0, 128),)),
        "norm_gain": jnp.clip(1.0 + 0.18 * jax.random.normal(key_of[6], (D,), jnp.float32), 0.1, 1.9),
        "router_weight": centred(key_of[7], (D, EXPERTS), D ** -0.5, 0.09375),
        "expert_ids": draw_expert_ids(jax.random.fold_in(jax.random.fold_in(key_of[12], part), 71), part),
        "gate_weight": centred(key_of[9], (FLIGHT, D, FFW), D ** -0.5, 0.09375, ((0, 4), (2, 32))),
        "up_weight": centred(key_of[10], (FLIGHT, D, FFW), D ** -0.5, 0.09375, ((0, 4), (2, 32))),
        "down_weight": centred(key_of[11], (FLIGHT, FFW, D), FFW ** -0.5, 0.0546875, ((0, 4), (1, 32))),
    }


def reference(head_inputs, input_matrix, output_matrix, log_decay, skip_gain, residual, norm_gain, router_weight, expert_ids, gate_weight, up_weight, down_weight):
    spans = STRING_ELEMENTS // TOK_DEV
    inputs_spanned = head_inputs.reshape(spans, TOK_DEV, RECURRENT_PARTS, P_SIZE)
    writes = input_matrix.reshape(spans, TOK_DEV, N)
    reads = output_matrix.reshape(spans, TOK_DEV, N)
    decays = log_decay.reshape(RECURRENT_PARTS, spans, TOK_DEV).transpose(1, 0, 2)
    causal = jnp.arange(TOK_DEV)[:, None] >= jnp.arange(TOK_DEV)[None, :]

    def span_step(state, packed):
        inputs_here, write_here, read_here, decay_here = packed
        cumulative = jnp.cumsum(decay_here, axis=1)
        scores = jnp.dot(read_here, write_here.T, preferred_element_type=jnp.float32)
        spread = jnp.minimum(cumulative[:, :, None] - cumulative[:, None, :], 0.0)
        mixing = jnp.where(causal[None], jnp.exp(spread) * scores[None], 0.0).astype(jnp.bfloat16)
        within = jnp.einsum('hts,shp->thp', mixing.astype(jnp.float32), inputs_here.astype(jnp.float32))
        remain = jnp.exp(cumulative[:, -1:] - cumulative)
        weighted = (remain[:, :, None] * write_here.astype(jnp.float32)[None]).astype(jnp.bfloat16)
        local_state = jnp.einsum('shp,hsn->hpn', inputs_here.astype(jnp.float32), weighted.astype(jnp.float32))
        carried = jnp.einsum('tn,hpn->thp', read_here.astype(jnp.float32), state, precision=lax.Precision.HIGHEST)
        carried = carried * jnp.exp(cumulative).T[:, :, None]
        mixed = within + carried + skip_gain[None, :, None] * inputs_here.astype(jnp.float32)
        new_state = jnp.exp(cumulative[:, -1])[:, None, None] * state + local_state
        return (new_state, mixed.reshape(TOK_DEV, RECURRENT_PARTS * P_SIZE).astype(jnp.bfloat16))
    _, mamba_spans = lax.scan(span_step, jnp.zeros((RECURRENT_PARTS, P_SIZE, N), jnp.float32), (inputs_spanned, writes, reads, decays))
    mamba_out = mamba_spans.reshape(STRING_ELEMENTS, D)
    stream = (residual.astype(jnp.float32) + mamba_out.astype(jnp.float32)).astype(jnp.bfloat16)
    stream_wide = stream.astype(jnp.float32)
    normed = (stream_wide * lax.rsqrt(lax.optimization_barrier(jnp.mean(stream_wide * stream_wide, axis=-1, keepdims=True)) + 1e-06) * norm_gain).astype(jnp.bfloat16)
    logits = jnp.dot(normed, router_weight, preferred_element_type=jnp.float32)
    expert_iota = jnp.arange(EXPERTS).astype(jnp.int32)
    first = expert_ids[:, 0]
    second = expert_ids[:, 1]
    first_logit = lax.optimization_barrier(jnp.sum(jnp.where(expert_iota[None] == first[:, None], logits, 0.0), axis=-1))
    second_logit = lax.optimization_barrier(jnp.sum(jnp.where(expert_iota[None] == second[:, None], logits, 0.0), axis=-1))
    gate = jax.nn.sigmoid(first_logit - second_logit)
    blocks = STRING_ELEMENTS // ROWS
    firsts = first.reshape(blocks, ROWS)
    member = (firsts[:, :, None] == jnp.arange(FLIGHT).astype(jnp.int32)[None, None, :]).astype(jnp.int32)
    ranking = jnp.cumsum(member, axis=1) - member
    slots = lax.optimization_barrier(jnp.sum(ranking * member, axis=-1))
    chosen = (member.transpose(0, 2, 1)[:, :, None, :] == 1) & (slots[:, None, None, :] == jnp.arange(CAP).astype(jnp.int32)[None, None, :, None])
    select = chosen.astype(jnp.float32)
    block_rows = normed.reshape(blocks, ROWS, D).astype(jnp.float32)
    outbound = jnp.einsum('becr,brd->ebcd', select, block_rows).astype(jnp.bfloat16).reshape(FLIGHT, blocks * CAP, D)
    group_units = FFW // N_SEQ

    def expert(packed):
        routed, gate_part, up_part, down_part = packed
        gated = jnp.dot(routed, gate_part, preferred_element_type=jnp.float32)
        lifted = jnp.dot(routed, up_part, preferred_element_type=jnp.float32)
        hidden = (jax.nn.silu(gated) * lifted).astype(jnp.bfloat16)
        groups = hidden.reshape(routed.shape[0], N_SEQ, group_units).transpose(1, 0, 2)
        down_groups = down_part.reshape(N_SEQ, group_units, D)

        def accumulate(total, pair):
            partial_sum = jnp.dot(pair[0], pair[1], preferred_element_type=jnp.float32).astype(jnp.bfloat16)
            return (total + lax.optimization_barrier(partial_sum).astype(jnp.float32), None)
        total, _ = lax.scan(accumulate, jnp.zeros((routed.shape[0], D), jnp.float32), (groups, down_groups))
        return total.astype(jnp.bfloat16)
    expert_out = lax.map(expert, (outbound, gate_weight, up_weight, down_weight))
    returned = expert_out.reshape(FLIGHT, blocks, CAP, D).astype(jnp.float32)
    combined = jnp.einsum('becr,ebcd->brd', select, returned).reshape(STRING_ELEMENTS, D)
    return (stream_wide + gate[:, None] * combined).astype(jnp.bfloat16)
```

```python
import functools

import jax
import jax.numpy as jnp
from jax import lax
from jax.experimental import pallas as pl
from jax.experimental.pallas import tpu as pltpu
from jax.sharding import PartitionSpec as P

MESH = pl.DeviceIdType.MESH
BF16 = jnp.bfloat16
F32 = jnp.float32
HIGH = lax.Precision.HIGHEST
P_SIZE = 64
CAP = 8
ROWS = 64
RUN_CAP = 16
NX = 4
NY = 4
NZ = 8
SEQ = NY * NZ
CONTRACT_ROWS = (((0,), (0,)), ((), ()))
CONTRACT_COLS = (((1,), (1,)), ((), ()))


def iota(shape, axis):
    return lax.broadcasted_iota(jnp.int32, shape, axis)


def block_select(first_row, experts, slots_each):
    shape = (experts * slots_each, ROWS)
    row_expert = iota(shape, 0) // slots_each
    member = (first_row == row_expert).astype(F32)
    before = (iota((ROWS, ROWS), 0) < iota((ROWS, ROWS), 1)).astype(BF16)
    rank = jnp.dot(member.astype(BF16), before, preferred_element_type=F32)
    count = jnp.sum(member, axis=1, keepdims=True)
    return member, rank, count


def mamba_kernel(
    decay_ref, x_ref, b_ref, c_ref, skip_ref, residual_ref, ids_ref,
    out_ref, picked_ref, ids_out_ref,
    dec_send, dec_recv, s_send, s_recv, e_send, e_recv, acc, grow, r_send, r_recv, ids_all,
    sems, x_send_sems,
):
    me = lax.axis_index("seq")
    mx = lax.axis_index("exp")
    length = x_ref.shape[0]
    heads = decay_ref.shape[0]

    def seq_peer(i):
        q = i // NY
        dz = NZ // 2 + ((q + 1) // 2) * (1 - 2 * (q % 2))
        dy = NY - 1 - i % NY
        z = (me // NY + dz) % NZ
        y = (me % NY + dy) % NY
        return z * NY + y

    barrier = pltpu.get_barrier_semaphore()

    def greet(i, carry):
        pl.semaphore_signal(barrier, inc=1, device_id={"seq": seq_peer(i)}, device_id_type=MESH)
        return carry

    lax.fori_loop(0, SEQ - 1, greet, 0)
    for d in range(1, NX):
        pl.semaphore_signal(barrier, inc=1, device_id={"exp": (mx + d) % NX}, device_id_type=MESH)

    decay = decay_ref[...]
    upper = (iota((length, length), 0) <= iota((length, length), 1)).astype(F32)
    cum = jnp.dot(decay, upper, preferred_element_type=F32, precision=HIGH)
    lower = (iota((length, length), 0) >= iota((length, length), 1)).astype(F32)
    cum_t = lax.dot_general(lower, decay, CONTRACT_COLS, preferred_element_type=F32, precision=HIGH)
    total = jnp.exp(jnp.broadcast_to(cum[:, length - 1 : length], (heads, 128)))
    for h in range(heads):
        dec_send[h] = total[h : h + 1, :]
    left = iota((length, 2 * P_SIZE), 1) < P_SIZE

    def spread(columns, i):
        wide = (length, 2 * P_SIZE)
        a = jnp.broadcast_to(columns[:, 2 * i : 2 * i + 1], wide)
        b = jnp.broadcast_to(columns[:, 2 * i + 1 : 2 * i + 2], wide)
        return jnp.where(left, a, b)

    remain = jnp.exp(cum_t[length - 1 : length, :] - cum_t)
    for i in range(heads // 2):
        pair = slice(128 * i, 128 * i + 128)
        weighted = (x_ref[:, pair].astype(F32) * spread(remain, i)).astype(BF16)
        state = lax.dot_general(weighted, b_ref[...], CONTRACT_ROWS, preferred_element_type=F32)
        s_send[4 * i : 4 * i + 4] = state.astype(BF16).reshape(4, 32, 128)

    pl.semaphore_wait(barrier, SEQ - 1 + NX - 1)

    def scatter(i, carry):
        j = seq_peer(i)
        pltpu.make_async_remote_copy(
            src_ref=s_send.at[j], dst_ref=s_recv.at[me], send_sem=sems.at[0], recv_sem=sems.at[1],
            device_id={"seq": j}, device_id_type=MESH,
        ).start()
        pltpu.make_async_remote_copy(
            src_ref=dec_send.at[j // 2], dst_ref=dec_recv.at[me], send_sem=sems.at[2], recv_sem=sems.at[3],
            device_id={"seq": j}, device_id_type=MESH,
        ).start()
        return carry

    lax.fori_loop(0, SEQ - 1, scatter, 0)
    s_recv[me] = s_send[me]
    dec_recv[me] = dec_send[me // 2]

    ids = ids_ref[...]
    member, rank, _ = block_select(ids[0:1, :ROWS], NX, CAP)
    slot = (iota((NX * CAP, ROWS), 0) % CAP).astype(F32)
    select = jnp.where(rank == slot, member, 0.0).astype(BF16)
    rows = jnp.dot(select, residual_ref[...], preferred_element_type=F32)
    r_send[...] = rows.astype(BF16).reshape(NX, CAP, residual_ref.shape[1])
    for d in range(1, NX):
        to = (mx + d) % NX
        pltpu.make_async_remote_copy(
            src_ref=r_send.at[to], dst_ref=r_recv.at[mx], send_sem=x_send_sems.at[0], recv_sem=sems.at[6],
            device_id={"exp": to}, device_id_type=MESH,
        ).start()
        pltpu.make_async_remote_copy(
            src_ref=ids_ref, dst_ref=ids_all.at[mx], send_sem=x_send_sems.at[1], recv_sem=sems.at[7],
            device_id={"exp": to}, device_id_type=MESH,
        ).start()
    r_recv[mx] = r_send[mx]
    ids_all[mx] = ids

    scores = lax.dot_general(c_ref[...], b_ref[...], CONTRACT_COLS, preferred_element_type=F32)
    scores = jnp.where(iota(scores.shape, 0) >= iota(scores.shape, 1), scores, 0.0)
    grown = jnp.exp(cum_t)
    for i in range(heads // 2):
        pair = slice(128 * i, 128 * i + 128)
        x_pair = x_ref[:, pair]
        parts = []
        for h in (2 * i, 2 * i + 1):
            gap = jnp.minimum(cum_t[:, h : h + 1] - cum[h : h + 1, :], 0.0)
            mixing = (jnp.exp(gap) * scores).astype(BF16)
            parts.append(jnp.dot(mixing, x_pair, preferred_element_type=F32))
        own = jnp.where(left, parts[0], parts[1])
        acc[:, pair] = own + skip_ref[:, pair] * x_pair.astype(F32)
        grow[:, pair] = spread(grown, i)

    def drain(ref, sem):
        pltpu.make_async_copy(ref, ref, sem).wait()

    drain(dec_recv.at[pl.ds(0, SEQ - 1)], sems.at[3])
    drain(s_recv.at[pl.ds(0, SEQ - 1)], sems.at[1])
    entering = jnp.zeros((32, 128), F32)
    for k in range(SEQ):
        e_send[k] = entering.astype(BF16)
        if k < SEQ - 1:
            entering = entering * dec_recv[k] + s_recv[k].astype(F32)

    def gather(i, carry):
        j = seq_peer(i)
        pltpu.make_async_remote_copy(
            src_ref=e_send.at[j], dst_ref=e_recv.at[me], send_sem=sems.at[4], recv_sem=sems.at[5],
            device_id={"seq": j}, device_id_type=MESH,
        ).start()
        return carry

    lax.fori_loop(0, SEQ - 1, gather, 0)
    e_recv[me] = e_send[me]

    drain(r_recv.at[pl.ds(0, NX - 1)], sems.at[6])
    drain(ids_all.at[pl.ds(0, NX - 1)], sems.at[7])
    picked_ref[...] = r_recv[...].reshape(picked_ref.shape)
    ids_out_ref[...] = ids_all[...]

    drain(e_recv.at[pl.ds(0, SEQ - 1)], sems.at[5])
    for i in range(heads // 2):
        pair = slice(128 * i, 128 * i + 128)
        carried = lax.dot_general(
            c_ref[...], e_recv[4 * i : 4 * i + 4].reshape(128, 128), CONTRACT_COLS, preferred_element_type=F32
        )
        out_ref[:, pair] = (acc[:, pair] + grow[:, pair] * carried).astype(BF16)

    drain(s_send.at[pl.ds(0, SEQ - 1)], sems.at[0])
    drain(dec_recv.at[pl.ds(0, SEQ - 1)], sems.at[2])
    drain(e_send.at[pl.ds(0, SEQ - 1)], sems.at[4])
    drain(r_send.at[pl.ds(0, NX - 1)], x_send_sems.at[0])
    drain(ids_all.at[pl.ds(0, NX - 1)], x_send_sems.at[1])


def mamba(x, b, c, decay, skip_row, residual, ids_rows):
    length, width = x.shape
    heads = decay.shape[0]
    d = residual.shape[1]
    vmem = pl.BlockSpec(memory_space=pltpu.VMEM)
    return pl.pallas_call(
        mamba_kernel,
        out_shape=(
            jax.ShapeDtypeStruct((length, width), BF16),
            jax.ShapeDtypeStruct((NX * CAP, d), BF16),
            jax.ShapeDtypeStruct((NX, 8, 128), jnp.int32),
        ),
        in_specs=[vmem] * 7,
        out_specs=(vmem, vmem, vmem),
        scratch_shapes=[
            pltpu.VMEM((heads, 1, 128), F32),
            pltpu.VMEM((SEQ, 1, 128), F32),
            pltpu.VMEM((SEQ, 32, 128), BF16),
            pltpu.VMEM((SEQ, 32, 128), BF16),
            pltpu.VMEM((SEQ, 32, 128), BF16),
            pltpu.VMEM((SEQ, 32, 128), BF16),
            pltpu.VMEM((length, width), F32),
            pltpu.VMEM((length, width), F32),
            pltpu.VMEM((NX, CAP, d), BF16),
            pltpu.VMEM((NX, CAP, d), BF16),
            pltpu.VMEM((NX, 8, 128), jnp.int32),
            pltpu.SemaphoreType.DMA((8,)),
            pltpu.SemaphoreType.DMA((2,)),
        ],
        compiler_params=pltpu.CompilerParams(collective_id=0, has_side_effects=True),
        name="mamba",
    )(decay, x, b, c, skip_row, residual, ids_rows)


def body(
    head_inputs, input_matrix, output_matrix, log_decay, skip_gain, residual, norm_gain,
    router_weight, expert_ids, gate_weight, up_weight, down_weight,
):
    skip_row = jnp.repeat(skip_gain, P_SIZE)[None, :]
    ids_rows = jnp.pad(expert_ids.T, ((0, 6), (0, 64)), constant_values=99)
    mamba_out, picked, ids_all = mamba(
        head_inputs, input_matrix, output_matrix, log_decay, skip_row, residual, ids_rows
    )
    token_rows = lax.all_to_all(mamba_out, "exp", split_axis=0, concat_axis=1, tiled=True)
    stream = (residual.astype(jnp.float32) + token_rows.astype(jnp.float32)).astype(jnp.bfloat16)
    stream_wide = stream.astype(jnp.float32)
    normed = (
        stream_wide
        * lax.rsqrt(jnp.mean(stream_wide * stream_wide, axis=-1, keepdims=True) + 1e-06)
        * norm_gain
    ).astype(jnp.bfloat16)
    logits = jnp.dot(normed, router_weight, preferred_element_type=jnp.float32)
    expert_iota = lax.broadcasted_iota(jnp.int32, logits.shape, 1)
    first = expert_ids[:, 0]
    second = expert_ids[:, 1]
    first_logit = jnp.sum(jnp.where(expert_iota == first[:, None], logits, 0.0), axis=-1)
    second_logit = jnp.sum(jnp.where(expert_iota == second[:, None], logits, 0.0), axis=-1)
    gate = jax.nn.sigmoid(first_logit - second_logit)
    flight = lax.axis_size("exp")
    member = (first[:, None] == jnp.arange(flight, dtype=jnp.int32)[None, :]).astype(jnp.int32)
    ranking = jnp.cumsum(member, axis=0) - member
    slots = jnp.sum(ranking * member, axis=-1)
    chosen = (member.T[:, None, :] == 1) & (
        slots[None, None, :] == jnp.arange(CAP, dtype=jnp.int32)[None, :, None]
    )
    select = chosen.astype(jnp.bfloat16)
    outbound = jnp.einsum("ecr,rd->ecd", select, normed, preferred_element_type=jnp.float32).astype(
        jnp.bfloat16
    )
    model_width = outbound.shape[2]
    inbound = lax.all_to_all(outbound, "exp", split_axis=0, concat_axis=0, tiled=True)
    routed = inbound.reshape(flight * CAP, model_width)
    fragment = lax.all_gather(routed, "seq", axis=0, tiled=True)
    gated = jnp.dot(fragment, gate_weight[0], preferred_element_type=jnp.float32)
    lifted = jnp.dot(fragment, up_weight[0], preferred_element_type=jnp.float32)
    hidden_all = (jax.nn.silu(gated) * lifted).astype(jnp.bfloat16)
    summed = lax.psum_scatter(
        jnp.dot(hidden_all, down_weight[0], preferred_element_type=jnp.float32).astype(jnp.bfloat16),
        "seq",
        scatter_dimension=0,
        tiled=True,
    )
    expert_out = summed.reshape(flight, CAP, model_width)
    returned = lax.all_to_all(expert_out, "exp", split_axis=0, concat_axis=0, tiled=True)
    combined = jnp.einsum("ecr,ecd->rd", select, returned, preferred_element_type=jnp.float32)
    return (stream_wide + gate[:, None] * combined).astype(jnp.bfloat16)


def solution(mesh):
    return jax.shard_map(
        body,
        mesh=mesh,
        in_specs=(
            P(("dp", "seq"), "exp"),
            P(("dp", "seq"), None),
            P(("dp", "seq"), None),
            P("exp", ("dp", "seq")),
            P("exp"),
            P(("dp", "seq", "exp"), None),
            P(),
            P(),
            P(("dp", "seq", "exp"), None),
            P("exp", None, "seq"),
            P("exp", None, "seq"),
            P("exp", "seq", None),
        ),
        out_specs=P(("dp", "seq", "exp"), None),
        check_vma=False,
    )
```

```python
import functools

import jax
import jax.numpy as jnp
from jax import lax
from jax.experimental import pallas as pl
from jax.experimental.pallas import tpu as pltpu
from jax.sharding import PartitionSpec as P

MESH = pl.DeviceIdType.MESH
BF16 = jnp.bfloat16
F32 = jnp.float32
HIGH = lax.Precision.HIGHEST
P_SIZE = 64
CAP = 8
ROWS = 64
RUN_CAP = 16
NX = 4
NY = 4
NZ = 8
SEQ = NY * NZ
CONTRACT_ROWS = (((0,), (0,)), ((), ()))
CONTRACT_COLS = (((1,), (1,)), ((), ()))


def iota(shape, axis):
    return lax.broadcasted_iota(jnp.int32, shape, axis)


def block_select(first_row, experts, slots_each):
    shape = (experts * slots_each, ROWS)
    row_expert = iota(shape, 0) // slots_each
    member = (first_row == row_expert).astype(F32)
    before = (iota((ROWS, ROWS), 0) < iota((ROWS, ROWS), 1)).astype(BF16)
    rank = jnp.dot(member.astype(BF16), before, preferred_element_type=F32)
    count = jnp.sum(member, axis=1, keepdims=True)
    return member, rank, count


def mamba_kernel(
    decay_ref, x_ref, b_ref, c_ref, skip_ref, residual_ref, ids_ref,
    out_ref, picked_ref, ids_out_ref,
    dec_send, dec_recv, s_send, s_recv, e_send, e_recv, acc, grow, r_send, r_recv, ids_all,
    sems, x_send_sems,
):
    me = lax.axis_index("seq")
    mx = lax.axis_index("exp")
    length = x_ref.shape[0]
    heads = decay_ref.shape[0]

    def seq_peer(i):
        q = i // NY
        dz = NZ // 2 + ((q + 1) // 2) * (1 - 2 * (q % 2))
        dy = NY - 1 - i % NY
        z = (me // NY + dz) % NZ
        y = (me % NY + dy) % NY
        return z * NY + y

    barrier = pltpu.get_barrier_semaphore()

    def greet(i, carry):
        pl.semaphore_signal(barrier, inc=1, device_id={"seq": seq_peer(i)}, device_id_type=MESH)
        return carry

    lax.fori_loop(0, SEQ - 1, greet, 0)
    for d in range(1, NX):
        pl.semaphore_signal(barrier, inc=1, device_id={"exp": (mx + d) % NX}, device_id_type=MESH)

    decay = decay_ref[...]
    upper = (iota((length, length), 0) <= iota((length, length), 1)).astype(F32)
    cum = jnp.dot(decay, upper, preferred_element_type=F32, precision=HIGH)
    lower = (iota((length, length), 0) >= iota((length, length), 1)).astype(F32)
    cum_t = lax.dot_general(lower, decay, CONTRACT_COLS, preferred_element_type=F32, precision=HIGH)
    total = jnp.exp(jnp.broadcast_to(cum[:, length - 1 : length], (heads, 128)))
    for h in range(heads):
        dec_send[h] = total[h : h + 1, :]
    left = iota((length, 2 * P_SIZE), 1) < P_SIZE

    def spread(columns, i):
        wide = (length, 2 * P_SIZE)
        a = jnp.broadcast_to(columns[:, 2 * i : 2 * i + 1], wide)
        b = jnp.broadcast_to(columns[:, 2 * i + 1 : 2 * i + 2], wide)
        return jnp.where(left, a, b)

    remain = jnp.exp(cum_t[length - 1 : length, :] - cum_t)
    for i in range(heads // 2):
        pair = slice(128 * i, 128 * i + 128)
        weighted = (x_ref[:, pair].astype(F32) * spread(remain, i)).astype(BF16)
        state = lax.dot_general(weighted, b_ref[...], CONTRACT_ROWS, preferred_element_type=F32)
        s_send[4 * i : 4 * i + 4] = state.astype(BF16).reshape(4, 32, 128)

    pl.semaphore_wait(barrier, SEQ - 1 + NX - 1)

    def scatter(i, carry):
        j = seq_peer(i)
        pltpu.make_async_remote_copy(
            src_ref=s_send.at[j], dst_ref=s_recv.at[me], send_sem=sems.at[0], recv_sem=sems.at[1],
            device_id={"seq": j}, device_id_type=MESH,
        ).start()
        pltpu.make_async_remote_copy(
            src_ref=dec_send.at[j // 2], dst_ref=dec_recv.at[me], send_sem=sems.at[2], recv_sem=sems.at[3],
            device_id={"seq": j}, device_id_type=MESH,
        ).start()
        return carry

    lax.fori_loop(0, SEQ - 1, scatter, 0)
    s_recv[me] = s_send[me]
    dec_recv[me] = dec_send[me // 2]

    ids = ids_ref[...]
    member, rank, _ = block_select(ids[0:1, :ROWS], NX, CAP)
    slot = (iota((NX * CAP, ROWS), 0) % CAP).astype(F32)
    select = jnp.where(rank == slot, member, 0.0).astype(BF16)
    rows = jnp.dot(select, residual_ref[...], preferred_element_type=F32)
    r_send[...] = rows.astype(BF16).reshape(NX, CAP, residual_ref.shape[1])
    for d in range(1, NX):
        to = (mx + d) % NX
        pltpu.make_async_remote_copy(
            src_ref=r_send.at[to], dst_ref=r_recv.at[mx], send_sem=x_send_sems.at[0], recv_sem=sems.at[6],
            device_id={"exp": to}, device_id_type=MESH,
        ).start()
        pltpu.make_async_remote_copy(
            src_ref=ids_ref, dst_ref=ids_all.at[mx], send_sem=x_send_sems.at[1], recv_sem=sems.at[7],
            device_id={"exp": to}, device_id_type=MESH,
        ).start()
    r_recv[mx] = r_send[mx]
    ids_all[mx] = ids

    scores = lax.dot_general(c_ref[...], b_ref[...], CONTRACT_COLS, preferred_element_type=F32)
    scores = jnp.where(iota(scores.shape, 0) >= iota(scores.shape, 1), scores, 0.0)
    grown = jnp.exp(cum_t)
    for i in range(heads // 2):
        pair = slice(128 * i, 128 * i + 128)
        x_pair = x_ref[:, pair]
        parts = []
        for h in (2 * i, 2 * i + 1):
            gap = jnp.minimum(cum_t[:, h : h + 1] - cum[h : h + 1, :], 0.0)
            mixing = (jnp.exp(gap) * scores).astype(BF16)
            parts.append(jnp.dot(mixing, x_pair, preferred_element_type=F32))
        own = jnp.where(left, parts[0], parts[1])
        acc[:, pair] = own + skip_ref[:, pair] * x_pair.astype(F32)
        grow[:, pair] = spread(grown, i)

    def drain(ref, sem):
        pltpu.make_async_copy(ref, ref, sem).wait()

    drain(dec_recv.at[pl.ds(0, SEQ - 1)], sems.at[3])
    drain(s_recv.at[pl.ds(0, SEQ - 1)], sems.at[1])
    entering = jnp.zeros((32, 128), F32)
    for k in range(SEQ):
        e_send[k] = entering.astype(BF16)
        if k < SEQ - 1:
            entering = entering * dec_recv[k] + s_recv[k].astype(F32)

    def gather(i, carry):
        j = seq_peer(i)
        pltpu.make_async_remote_copy(
            src_ref=e_send.at[j], dst_ref=e_recv.at[me], send_sem=sems.at[4], recv_sem=sems.at[5],
            device_id={"seq": j}, device_id_type=MESH,
        ).start()
        return carry

    lax.fori_loop(0, SEQ - 1, gather, 0)
    e_recv[me] = e_send[me]

    drain(r_recv.at[pl.ds(0, NX - 1)], sems.at[6])
    drain(ids_all.at[pl.ds(0, NX - 1)], sems.at[7])
    picked_ref[...] = r_recv[...].reshape(picked_ref.shape)
    ids_out_ref[...] = ids_all[...]

    drain(e_recv.at[pl.ds(0, SEQ - 1)], sems.at[5])
    for i in range(heads // 2):
        pair = slice(128 * i, 128 * i + 128)
        carried = lax.dot_general(
            c_ref[...], e_recv[4 * i : 4 * i + 4].reshape(128, 128), CONTRACT_COLS, preferred_element_type=F32
        )
        out_ref[:, pair] = (acc[:, pair] + grow[:, pair] * carried).astype(BF16)

    drain(s_send.at[pl.ds(0, SEQ - 1)], sems.at[0])
    drain(dec_recv.at[pl.ds(0, SEQ - 1)], sems.at[2])
    drain(e_send.at[pl.ds(0, SEQ - 1)], sems.at[4])
    drain(r_send.at[pl.ds(0, NX - 1)], x_send_sems.at[0])
    drain(ids_all.at[pl.ds(0, NX - 1)], x_send_sems.at[1])


def mamba(x, b, c, decay, skip_row, residual, ids_rows):
    length, width = x.shape
    heads = decay.shape[0]
    d = residual.shape[1]
    vmem = pl.BlockSpec(memory_space=pltpu.VMEM)
    return pl.pallas_call(
        mamba_kernel,
        out_shape=(
            jax.ShapeDtypeStruct((length, width), BF16),
            jax.ShapeDtypeStruct((NX * CAP, d), BF16),
            jax.ShapeDtypeStruct((NX, 8, 128), jnp.int32),
        ),
        in_specs=[vmem] * 7,
        out_specs=(vmem, vmem, vmem),
        scratch_shapes=[
            pltpu.VMEM((heads, 1, 128), F32),
            pltpu.VMEM((SEQ, 1, 128), F32),
            pltpu.VMEM((SEQ, 32, 128), BF16),
            pltpu.VMEM((SEQ, 32, 128), BF16),
            pltpu.VMEM((SEQ, 32, 128), BF16),
            pltpu.VMEM((SEQ, 32, 128), BF16),
            pltpu.VMEM((length, width), F32),
            pltpu.VMEM((length, width), F32),
            pltpu.VMEM((NX, CAP, d), BF16),
            pltpu.VMEM((NX, CAP, d), BF16),
            pltpu.VMEM((NX, 8, 128), jnp.int32),
            pltpu.SemaphoreType.DMA((8,)),
            pltpu.SemaphoreType.DMA((2,)),
        ],
        compiler_params=pltpu.CompilerParams(collective_id=0, has_side_effects=True),
        name="mamba",
    )(decay, x, b, c, skip_row, residual, ids_rows)


SPLIT = 1664
P_PART = (0, 768, SPLIT)
Q_PART = (SPLIT, SPLIT + 1152, 4096)
HALF = NZ // 2


def expert_kernel(
    mixed_ref, picked_ref, ids_rows_ref, ids_ref, residual_ref, gain_ref, router_ref,
    gate_hbm, up_hbm, down_hbm,
    out_ref,
    gate_w, up_w, down_w, m_send, g_in, t_in, held, part, hidden, gated, lifted,
    pz_in, py_in, qy_in, qz_in, ret_send, ret_in, stream, gate_col, stream16, result,
    load_sems, send_sems, recv_sems,
):
    me = lax.axis_index("seq")
    mx = lax.axis_index("exp")
    z = me // NY
    y = me % NY
    d_model = residual_ref.shape[1]
    d_part = d_model // NX

    loads = [
        pltpu.make_async_copy(src.at[0], dst, load_sems.at[i])
        for i, (src, dst) in enumerate(((gate_hbm, gate_w), (up_hbm, up_w), (down_hbm, down_w)))
    ]
    for load in loads:
        load.start()

    ahead_z = {"seq": (z + 1) % NZ * NY + y}
    behind_z = {"seq": (z + NZ - 1) % NZ * NY + y}
    ahead_y = {"seq": z * NY + (y + 1) % NY}
    behind_y = {"seq": z * NY + (y + NY - 1) % NY}
    to_z = {1: ahead_z, -1: behind_z}
    to_y = {1: ahead_y, -1: behind_y}

    barrier = pltpu.get_barrier_semaphore()
    for neighbour in (ahead_z, behind_z, ahead_y, behind_y):
        pl.semaphore_signal(barrier, inc=1, device_id=neighbour, device_id_type=MESH)
    for d in range(1, NX):
        pl.semaphore_signal(barrier, inc=1, device_id={"exp": (mx + d) % NX}, device_id_type=MESH)

    copies = {}

    def send(key, src, dst, device):
        i = len(copies)
        copy = pltpu.make_async_remote_copy(
            src_ref=src, dst_ref=dst, send_sem=send_sems.at[i], recv_sem=recv_sems.at[i],
            device_id=device, device_id_type=MESH,
        )
        copies[key] = copy
        copy.start()

    def arrived(key):
        copies[key].wait_recv()

    offset = jnp.zeros((NX * RUN_CAP, 1), F32)
    slot = (iota((NX * RUN_CAP, ROWS), 0) % RUN_CAP).astype(F32)
    rows = jnp.zeros((NX * RUN_CAP, d_part), F32)
    pack_slot = iota((RUN_CAP, NX * CAP), 0)
    pack_block = iota((RUN_CAP, NX * CAP), 1) // CAP
    pack_place = iota((RUN_CAP, NX * CAP), 1) % CAP
    back_slot = iota((NX * CAP, RUN_CAP), 1)
    back_block = iota((NX * CAP, RUN_CAP), 0) // CAP
    back_place = iota((NX * CAP, RUN_CAP), 0) % CAP
    pack = jnp.zeros((RUN_CAP, NX * CAP), F32)
    back = jnp.zeros((NX * CAP, RUN_CAP), F32)
    mine = jnp.zeros((1, 1), F32)
    for b in range(NX):
        first_row = ids_rows_ref[b][0:1, :ROWS]
        member, rank, count = block_select(first_row, NX, RUN_CAP)
        select = jnp.where(rank + offset == slot, member, 0.0).astype(BF16)
        rows += jnp.dot(select, mixed_ref[ROWS * b : ROWS * b + ROWS, :], preferred_element_type=F32)
        offset += count
        here = jnp.sum((first_row == mx).astype(F32), axis=1, keepdims=True)

        def match(of_block, of_place, of_slot):
            place = of_place.astype(F32)
            hit = (of_block == b) & (place < here) & (place + mine == of_slot.astype(F32))
            return hit.astype(F32)

        pack += match(pack_block, pack_place, pack_slot)
        back += match(back_block, back_place, back_slot)
        mine += here
    m_send[...] = rows.astype(BF16).reshape(NX, RUN_CAP, d_part)

    pl.semaphore_wait(barrier, 4 + NX - 1)
    for d in range(1, NX):
        to = (mx + d) % NX
        send(("row", d), m_send.at[to], g_in.at[mx], {"exp": to})
    for d in range(1, NX):
        to = (mx + d) % NX
        start_row = pl.multiple_of(to * ROWS, ROWS)
        send(("token", d), mixed_ref.at[pl.ds(start_row, ROWS), :], t_in.at[mx], {"exp": to})
    g_in[mx] = m_send[mx]
    t_in[mx] = mixed_ref[pl.ds(pl.multiple_of(mx * ROWS, ROWS), ROWS), :]

    gain = gain_ref[...]

    def normalize(wide):
        return (wide * lax.rsqrt(jnp.mean(wide * wide, axis=-1, keepdims=True) + 1e-06) * gain).astype(BF16)

    stream16[...] = jnp.dot(pack.astype(BF16), picked_ref[...], preferred_element_type=F32)
    for d in range(1, NX):
        arrived(("row", d))
    for i in range(NX):
        cols = slice(d_part * i, d_part * i + d_part)
        stream16[:, cols] = (stream16[:, cols] + g_in[i].astype(F32)).astype(BF16).astype(F32)
    held[z, y] = normalize(stream16[...])

    whole_p = pl.ds(P_PART[0], P_PART[2] - P_PART[0])
    whole_q = pl.ds(Q_PART[0], Q_PART[2] - Q_PART[0])
    p_cols = (pl.ds(P_PART[0], P_PART[1] - P_PART[0]), pl.ds(P_PART[1], P_PART[2] - P_PART[1]))
    q_cols = (pl.ds(Q_PART[0], Q_PART[1] - Q_PART[0]), pl.ds(Q_PART[1], Q_PART[2] - Q_PART[1]))

    def far(way):
        return 0 if way == 1 else 1

    def pieces(way, distance, last):
        if distance == last:
            return (far(way),)
        return (far(way), 1 - far(way))

    def at_z(shift):
        return (z + shift + NZ) % NZ

    def at_y(shift):
        return (y + shift + NY) % NY

    def planes_of(distance):
        if distance == 0:
            return (0,)
        if distance == HALF:
            return (HALF,)
        return (-distance, distance)

    def share(key, ref, device):
        send(key, ref, ref, device)

    def q_round_y(plane):
        for way in (1, -1):
            share(("qy", plane, 1, way), held.at[at_z(plane), y, :, whole_q], to_y[way])

    def q_relay_y(plane):
        for way in (1, -1):
            arrived(("qy", plane, 1, way))
            share(("qy", plane, 2, way), held.at[at_z(plane), at_y(-way), :, q_cols[far(way)]], to_y[way])

    for way in (1, -1):
        share(("py", 1, way), held.at[z, y, :, whole_p], to_y[way])
        for piece in pieces(way, 1, HALF):
            share(("qz", 1, way, piece), held.at[z, y, :, q_cols[piece]], to_z[way])
    q_round_y(0)
    for way in (1, -1):
        arrived(("py", 1, way))
        share(("py", 2, way), held.at[z, at_y(-way), :, p_cols[far(way)]], to_y[way])
    q_relay_y(0)
    for way in (1, -1):
        arrived(("py", 2, way))
    for way in (1, -1):
        for piece in pieces(way, 1, HALF):
            share(("pz", 1, way, piece), held.at[z, :, :, p_cols[piece]], to_z[way])

    def own_tokens():
        for d in range(1, NX):
            arrived(("token", d))
        for i in range(NX):
            cols = slice(d_part * i, d_part * i + d_part)
            stream[:, cols] = (residual_ref[:, cols].astype(F32) + t_in[i].astype(F32)).astype(BF16)
        normed = normalize(stream[...].astype(F32))
        logits = jnp.dot(normed, router_ref[...], preferred_element_type=F32)
        experts = iota(logits.shape, 1)
        picks = [
            jnp.sum(jnp.where(experts == ids_ref[:, j : j + 1], logits, 0.0), axis=-1, keepdims=True)
            for j in range(2)
        ]
        gate_col[...] = jnp.broadcast_to(jax.nn.sigmoid(picks[0] - picks[1]), gate_col.shape)

    step_k = 512

    def compute(planes):
        for plane in planes:
            for way in (1, -1):
                arrived(("qy", plane, 2, way))
        count = len(planes) * NY * RUN_CAP
        gated[:count] = jnp.zeros((count, gated.shape[1]), F32)
        lifted[:count] = jnp.zeros((count, lifted.shape[1]), F32)

        def up_step(k, carry):
            depth = pl.ds(pl.multiple_of(k * step_k, step_k), step_k)
            blocks = [held[at_z(plane), :, :, depth].reshape(NY * RUN_CAP, step_k) for plane in planes]
            tokens = blocks[0] if len(blocks) == 1 else jnp.concatenate(blocks, axis=0)
            gated[:count] += jnp.dot(tokens, gate_w[depth, :], preferred_element_type=F32)
            lifted[:count] += jnp.dot(tokens, up_w[depth, :], preferred_element_type=F32)
            return carry

        lax.fori_loop(0, d_model // step_k, up_step, 0)
        hidden[:count] = (jax.nn.silu(gated[:count]) * lifted[:count]).astype(BF16)

        def down_step(n, carry):
            cols = pl.ds(pl.multiple_of(n * step_k, step_k), step_k)
            sums = jnp.dot(hidden[:count], down_w[:, cols], preferred_element_type=F32).astype(BF16)
            for i, plane in enumerate(planes):
                rows_of = sums[i * NY * RUN_CAP : (i + 1) * NY * RUN_CAP]
                part[at_z(plane), :, :, cols] = rows_of.reshape(NY, RUN_CAP, step_k)
            return carry

        lax.fori_loop(0, d_model // step_k, down_step, 0)

    for distance in range(1, HALF + 1):
        for way in (1, -1):
            for piece in pieces(way, distance, HALF):
                arrived(("qz", distance, way, piece))
                if distance < HALF and piece in pieces(way, distance + 1, HALF):
                    share(
                        ("qz", distance + 1, way, piece),
                        held.at[at_z(-way * distance), y, :, q_cols[piece]], to_z[way],
                    )
        for plane in planes_of(distance):
            q_round_y(plane)
        for way in (1, -1):
            for piece in pieces(way, distance, HALF):
                arrived(("pz", distance, way, piece))
                if distance < HALF and piece in pieces(way, distance + 1, HALF):
                    share(
                        ("pz", distance + 1, way, piece),
                        held.at[at_z(-way * distance), :, :, p_cols[piece]], to_z[way],
                    )
        for plane in planes_of(distance):
            q_relay_y(plane)
        if distance == 1:
            own_tokens()
            for load in loads:
                load.wait()
        compute(planes_of(distance - 1))

    def add(where, piece_in):
        total = part[where].astype(F32) + piece_in.astype(F32)
        part[where] = total.astype(BF16)

    def q_sum_start(plane):
        for way in (1, -1):
            cols = q_cols[far(way)]
            send(
                ("rqy", plane, 2, way), part.at[at_z(plane), at_y(2 * way), :, cols],
                qy_in.at[plane + HALF - 1, far(way), 1, :, pl.ds(cols.start - SPLIT, cols.size)], to_y[way],
            )

    def q_sum_relay(plane):
        for way in (1, -1):
            cols = q_cols[far(way)]
            arrived(("rqy", plane, 2, way))
            add(
                (at_z(plane), at_y(way), slice(None), cols),
                qy_in[plane + HALF - 1, far(way), 1, :, pl.ds(cols.start - SPLIT, cols.size)],
            )
            send(
                ("rqy", plane, 1, way), part.at[at_z(plane), at_y(way), :, whole_q],
                qy_in.at[plane + HALF - 1, far(way), 0], to_y[way],
            )

    def q_sum_y(plane):
        for way in (1, -1):
            arrived(("rqy", plane, 1, way))
        total = part[at_z(plane), y, :, whole_q].astype(F32)
        total += qy_in[plane + HALF - 1, 0, 0].astype(F32) + qy_in[plane + HALF - 1, 1, 0].astype(F32)
        return total

    def p_send(distance):
        for way in (1, -1):
            for piece in pieces(way, distance, HALF):
                cols = p_cols[piece]
                if distance < HALF and piece in pieces(way, distance + 1, HALF):
                    arrived(("rpz", distance + 1, way, piece))
                    add((at_z(way * distance), slice(None), slice(None), cols), pz_in[far(way), distance, :, :, cols])
                send(
                    ("rpz", distance, way, piece), part.at[at_z(way * distance), :, :, cols],
                    pz_in.at[far(way), distance - 1, :, :, cols], to_z[way],
                )

    def q_send(distance):
        for plane in planes_of(distance):
            part[at_z(plane), y, :, whole_q] = q_sum_y(plane).astype(BF16)
        for way in (1, -1):
            for piece in pieces(way, distance, HALF):
                cols = q_cols[piece]
                inner = pl.ds(cols.start - SPLIT, cols.size)
                if distance < HALF and piece in pieces(way, distance + 1, HALF):
                    arrived(("rqz", distance + 1, way, piece))
                    add((at_z(way * distance), y, slice(None), cols), qz_in[far(way), distance, :, inner])
                send(
                    ("rqz", distance, way, piece), part.at[at_z(way * distance), y, :, cols],
                    qz_in.at[far(way), distance - 1, :, inner], to_z[way],
                )

    for distance in range(HALF - 1, -1, -1):
        for plane in planes_of(distance):
            q_sum_start(plane)
    compute(planes_of(HALF))
    for plane in planes_of(HALF):
        q_sum_start(plane)
    p_send(HALF)
    for distance in range(HALF, -1, -1):
        for plane in planes_of(distance):
            q_sum_relay(plane)
    q_send(HALF)
    for distance in range(HALF - 1, 0, -1):
        p_send(distance)
        q_send(distance)

    for way in (1, -1):
        for piece in pieces(way, 1, HALF):
            arrived(("rpz", 1, way, piece))
    sums = part[z, :, :, whole_p].astype(F32) + pz_in[0, 0].astype(F32) + pz_in[1, 0].astype(F32)
    part[z, :, :, whole_p] = sums.astype(BF16)
    for way in (1, -1):
        cols = p_cols[far(way)]
        send(("rpy", 2, way), part.at[z, at_y(2 * way), :, cols], py_in.at[far(way), 1, :, cols], to_y[way])

    def give_back(cols, name):
        give = jnp.dot(back.astype(BF16), result[:, cols], preferred_element_type=F32)
        ret_send[:, :, cols] = give.astype(BF16).reshape(NX, CAP, cols.size)
        for d in range(1, NX):
            to = (mx + d) % NX
            send((name, d), ret_send.at[to, :, cols], ret_in.at[mx, :, cols], {"exp": to})
        ret_in[mx, :, cols] = ret_send[mx, :, cols]

    total = q_sum_y(0)
    for way in (1, -1):
        arrived(("rpy", 2, way))
        cols = p_cols[far(way)]
        add((z, at_y(way), slice(None), cols), py_in[far(way), 1, :, cols])
        send(("rpy", 1, way), part.at[z, at_y(way), :, whole_p], py_in.at[far(way), 0], to_y[way])
    for way in (1, -1):
        for piece in pieces(way, 1, HALF):
            arrived(("rqz", 1, way, piece))
    total += qz_in[0, 0].astype(F32) + qz_in[1, 0].astype(F32)
    result[:, whole_q] = total.astype(BF16)
    give_back(whole_q, "back_q")
    for way in (1, -1):
        arrived(("rpy", 1, way))
    total = part[z, y, :, whole_p].astype(F32) + py_in[0, 0].astype(F32) + py_in[1, 0].astype(F32)
    result[:, whole_p] = total.astype(BF16)
    give_back(whole_p, "back_p")

    own_expert = iota((ROWS, NX * CAP), 1) // CAP
    own_slot = iota((ROWS, NX * CAP), 1) % CAP
    member = (ids_ref[:, 0:1] == own_expert).astype(F32)
    before = (iota((ROWS, ROWS), 1) < iota((ROWS, ROWS), 0)).astype(BF16)
    rank = jnp.dot(before, member.astype(BF16), preferred_element_type=F32)
    select = jnp.where(rank == own_slot.astype(F32), member, 0.0).astype(BF16)
    for name, cols in (("back_q", whole_q), ("back_p", whole_p)):
        for d in range(1, NX):
            arrived((name, d))
        combined = jnp.dot(select, ret_in[:, :, cols].reshape(NX * CAP, cols.size), preferred_element_type=F32)
        out_ref[:, cols] = (stream[:, cols].astype(F32) + gate_col[:, 0:1] * combined).astype(BF16)
    for copy in copies.values():
        copy.wait_send()


def experts(mixed, picked, ids_rows, ids, residual, gain, router, gate_weight, up_weight, down_weight):
    rows, d = residual.shape
    units = gate_weight.shape[2]
    d_part = mixed.shape[1]
    vmem = pl.BlockSpec(memory_space=pltpu.VMEM)
    hbm = pl.BlockSpec(memory_space=pl.ANY)
    p_width, q_width = SPLIT, d - SPLIT
    return pl.pallas_call(
        expert_kernel,
        out_shape=jax.ShapeDtypeStruct((rows, d), BF16),
        in_specs=[vmem] * 7 + [hbm] * 3,
        out_specs=vmem,
        scratch_shapes=[
            pltpu.VMEM((d, units), BF16),
            pltpu.VMEM((d, units), BF16),
            pltpu.VMEM((units, d), BF16),
            pltpu.VMEM((NX, RUN_CAP, d_part), BF16),
            pltpu.VMEM((NX, RUN_CAP, d_part), BF16),
            pltpu.VMEM((NX, ROWS, d_part), BF16),
            pltpu.VMEM((NZ, NY, RUN_CAP, d), BF16),
            pltpu.VMEM((NZ, NY, RUN_CAP, d), BF16),
            pltpu.VMEM((2 * NY * RUN_CAP, units), BF16),
            pltpu.VMEM((2 * NY * RUN_CAP, units), F32),
            pltpu.VMEM((2 * NY * RUN_CAP, units), F32),
            pltpu.VMEM((2, HALF, NY, RUN_CAP, p_width), BF16),
            pltpu.VMEM((2, 2, RUN_CAP, p_width), BF16),
            pltpu.VMEM((NZ, 2, 2, RUN_CAP, q_width), BF16),
            pltpu.VMEM((2, HALF, RUN_CAP, q_width), BF16),
            pltpu.VMEM((NX, CAP, d), BF16),
            pltpu.VMEM((NX, CAP, d), BF16),
            pltpu.VMEM((rows, d), BF16),
            pltpu.VMEM((rows, 128), F32),
            pltpu.VMEM((RUN_CAP, d), F32),
            pltpu.VMEM((RUN_CAP, d), BF16),
            pltpu.SemaphoreType.DMA((3,)),
            pltpu.SemaphoreType.DMA((160,)),
            pltpu.SemaphoreType.DMA((160,)),
        ],
        compiler_params=pltpu.CompilerParams(
            collective_id=1, has_side_effects=True, vmem_limit_bytes=60 * 1024 * 1024
        ),
        name="experts",
    )(mixed, picked, ids_rows, ids, residual, gain, router, gate_weight, up_weight, down_weight)


def body(
    head_inputs, input_matrix, output_matrix, log_decay, skip_gain, residual, norm_gain,
    router_weight, expert_ids, gate_weight, up_weight, down_weight,
):
    skip_row = jnp.repeat(skip_gain, P_SIZE)[None, :]
    ids_rows = jnp.pad(expert_ids.T, ((0, 6), (0, 64)), constant_values=99)
    mixed, picked, ids_all = mamba(
        head_inputs, input_matrix, output_matrix, log_decay, skip_row, residual, ids_rows
    )
    return experts(
        mixed, picked, ids_all, expert_ids, residual, norm_gain[None, :], router_weight,
        gate_weight, up_weight, down_weight,
    )


def solution(mesh):
    return jax.shard_map(
        body,
        mesh=mesh,
        in_specs=(
            P(("dp", "seq"), "exp"),
            P(("dp", "seq"), None),
            P(("dp", "seq"), None),
            P("exp", ("dp", "seq")),
            P("exp"),
            P(("dp", "seq", "exp"), None),
            P(),
            P(),
            P(("dp", "seq", "exp"), None),
            P("exp", None, "seq"),
            P("exp", None, "seq"),
            P("exp", "seq", None),
        ),
        out_specs=P(("dp", "seq", "exp"), None),
        check_vma=False,
    )
```

```python
import functools

import jax
import jax.numpy as jnp
from jax import lax
from jax.experimental import pallas as pl
from jax.experimental.pallas import tpu as pltpu
from jax.sharding import PartitionSpec as P

MESH = pl.DeviceIdType.MESH
BF16 = jnp.bfloat16
F32 = jnp.float32
HIGH = lax.Precision.HIGHEST
P_SIZE = 64
CAP = 8
ROWS = 64
RUN_CAP = 16
NX = 4
NY = 4
NZ = 8
SEQ = NY * NZ
CONTRACT_ROWS = (((0,), (0,)), ((), ()))
CONTRACT_COLS = (((1,), (1,)), ((), ()))


def iota(shape, axis):
    return lax.broadcasted_iota(jnp.int32, shape, axis)


def block_select(first_row, experts, slots_each):
    shape = (experts * slots_each, ROWS)
    row_expert = iota(shape, 0) // slots_each
    member = (first_row == row_expert).astype(F32)
    before = (iota((ROWS, ROWS), 0) < iota((ROWS, ROWS), 1)).astype(BF16)
    rank = jnp.dot(member.astype(BF16), before, preferred_element_type=F32)
    count = jnp.sum(member, axis=1, keepdims=True)
    return member, rank, count


def mamba_kernel(
    decay_ref, x_ref, b_ref, c_ref, skip_ref, residual_ref, ids_ref,
    out_ref, picked_ref, ids_out_ref,
    dec_send, dec_recv, s_send, s_recv, e_send, e_recv, acc, grow, r_send, r_recv, ids_all,
    sems, x_send_sems,
):
    me = lax.axis_index("seq")
    mx = lax.axis_index("exp")
    length = x_ref.shape[0]
    heads = decay_ref.shape[0]

    def seq_peer(i):
        q = i // NY
        dz = NZ // 2 + ((q + 1) // 2) * (1 - 2 * (q % 2))
        dy = NY - 1 - i % NY
        z = (me // NY + dz) % NZ
        y = (me % NY + dy) % NY
        return z * NY + y

    barrier = pltpu.get_barrier_semaphore()

    def greet(i, carry):
        pl.semaphore_signal(barrier, inc=1, device_id={"seq": seq_peer(i)}, device_id_type=MESH)
        return carry

    lax.fori_loop(0, SEQ - 1, greet, 0)
    for d in range(1, NX):
        pl.semaphore_signal(barrier, inc=1, device_id={"exp": (mx + d) % NX}, device_id_type=MESH)

    decay = decay_ref[...]
    upper = (iota((length, length), 0) <= iota((length, length), 1)).astype(F32)
    cum = jnp.dot(decay, upper, preferred_element_type=F32, precision=HIGH)
    lower = (iota((length, length), 0) >= iota((length, length), 1)).astype(F32)
    cum_t = lax.dot_general(lower, decay, CONTRACT_COLS, preferred_element_type=F32, precision=HIGH)
    total = jnp.exp(jnp.broadcast_to(cum[:, length - 1 : length], (heads, 128)))
    for h in range(heads):
        dec_send[h] = total[h : h + 1, :]
    left = iota((length, 2 * P_SIZE), 1) < P_SIZE

    def spread(columns, i):
        wide = (length, 2 * P_SIZE)
        a = jnp.broadcast_to(columns[:, 2 * i : 2 * i + 1], wide)
        b = jnp.broadcast_to(columns[:, 2 * i + 1 : 2 * i + 2], wide)
        return jnp.where(left, a, b)

    remain = jnp.exp(cum_t[length - 1 : length, :] - cum_t)
    for i in range(heads // 2):
        pair = slice(128 * i, 128 * i + 128)
        weighted = (x_ref[:, pair].astype(F32) * spread(remain, i)).astype(BF16)
        state = lax.dot_general(weighted, b_ref[...], CONTRACT_ROWS, preferred_element_type=F32)
        s_send[4 * i : 4 * i + 4] = state.astype(BF16).reshape(4, 32, 128)

    pl.semaphore_wait(barrier, SEQ - 1 + NX - 1)

    def scatter(i, carry):
        j = seq_peer(i)
        pltpu.make_async_remote_copy(
            src_ref=s_send.at[j], dst_ref=s_recv.at[me], send_sem=sems.at[0], recv_sem=sems.at[1],
            device_id={"seq": j}, device_id_type=MESH,
        ).start()
        pltpu.make_async_remote_copy(
            src_ref=dec_send.at[j // 2], dst_ref=dec_recv.at[me], send_sem=sems.at[2], recv_sem=sems.at[3],
            device_id={"seq": j}, device_id_type=MESH,
        ).start()
        return carry

    lax.fori_loop(0, SEQ - 1, scatter, 0)
    s_recv[me] = s_send[me]
    dec_recv[me] = dec_send[me // 2]

    ids = ids_ref[...]
    member, rank, _ = block_select(ids[0:1, :], NX, CAP)
    slot = (iota((NX * CAP, ROWS), 0) % CAP).astype(F32)
    select = jnp.where(rank == slot, member, 0.0).astype(BF16)
    rows = jnp.dot(select, residual_ref[...], preferred_element_type=F32)
    r_send[...] = rows.astype(BF16).reshape(NX, CAP, residual_ref.shape[1])
    for d in range(1, NX):
        to = (mx + d) % NX
        pltpu.make_async_remote_copy(
            src_ref=r_send.at[to], dst_ref=r_recv.at[mx], send_sem=x_send_sems.at[0], recv_sem=sems.at[6],
            device_id={"exp": to}, device_id_type=MESH,
        ).start()
        pltpu.make_async_remote_copy(
            src_ref=ids_ref, dst_ref=ids_all.at[mx], send_sem=x_send_sems.at[1], recv_sem=sems.at[7],
            device_id={"exp": to}, device_id_type=MESH,
        ).start()
    r_recv[mx] = r_send[mx]
    ids_all[mx] = ids

    scores = lax.dot_general(c_ref[...], b_ref[...], CONTRACT_COLS, preferred_element_type=F32)
    scores = jnp.where(iota(scores.shape, 0) >= iota(scores.shape, 1), scores, 0.0)
    grown = jnp.exp(cum_t)
    for i in range(heads // 2):
        pair = slice(128 * i, 128 * i + 128)
        x_pair = x_ref[:, pair]
        parts = []
        for h in (2 * i, 2 * i + 1):
            gap = jnp.minimum(cum_t[:, h : h + 1] - cum[h : h + 1, :], 0.0)
            mixing = (jnp.exp(gap) * scores).astype(BF16)
            parts.append(jnp.dot(mixing, x_pair, preferred_element_type=F32))
        own = jnp.where(left, parts[0], parts[1])
        gains = [jnp.broadcast_to(skip_ref[:, h : h + 1], (1, 2 * P_SIZE)) for h in (2 * i, 2 * i + 1)]
        acc[:, pair] = own + jnp.where(left[0:1], gains[0], gains[1]) * x_pair.astype(F32)
        grow[:, pair] = spread(grown, i)

    def drain(ref, sem):
        pltpu.make_async_copy(ref, ref, sem).wait()

    drain(dec_recv.at[pl.ds(0, SEQ - 1)], sems.at[3])
    drain(s_recv.at[pl.ds(0, SEQ - 1)], sems.at[1])
    entering = jnp.zeros((32, 128), F32)
    for k in range(SEQ):
        e_send[k] = entering.astype(BF16)
        if k < SEQ - 1:
            entering = entering * dec_recv[k] + s_recv[k].astype(F32)

    def gather(i, carry):
        j = seq_peer(i)
        pltpu.make_async_remote_copy(
            src_ref=e_send.at[j], dst_ref=e_recv.at[me], send_sem=sems.at[4], recv_sem=sems.at[5],
            device_id={"seq": j}, device_id_type=MESH,
        ).start()
        return carry

    lax.fori_loop(0, SEQ - 1, gather, 0)
    e_recv[me] = e_send[me]

    drain(r_recv.at[pl.ds(0, NX - 1)], sems.at[6])
    drain(ids_all.at[pl.ds(0, NX - 1)], sems.at[7])
    picked_ref[...] = r_recv[...].reshape(picked_ref.shape)
    ids_out_ref[...] = ids_all[...]

    drain(e_recv.at[pl.ds(0, SEQ - 1)], sems.at[5])
    for i in range(heads // 2):
        pair = slice(128 * i, 128 * i + 128)
        carried = lax.dot_general(
            c_ref[...], e_recv[4 * i : 4 * i + 4].reshape(128, 128), CONTRACT_COLS, preferred_element_type=F32
        )
        out_ref[:, pair] = (acc[:, pair] + grow[:, pair] * carried).astype(BF16)

    drain(s_send.at[pl.ds(0, SEQ - 1)], sems.at[0])
    drain(dec_recv.at[pl.ds(0, SEQ - 1)], sems.at[2])
    drain(e_send.at[pl.ds(0, SEQ - 1)], sems.at[4])
    drain(r_send.at[pl.ds(0, NX - 1)], x_send_sems.at[0])
    drain(ids_all.at[pl.ds(0, NX - 1)], x_send_sems.at[1])


def mamba(x, b, c, decay, skip_row, residual, ids_rows):
    length, width = x.shape
    heads = decay.shape[0]
    d = residual.shape[1]
    vmem = pl.BlockSpec(memory_space=pltpu.VMEM)
    return pl.pallas_call(
        mamba_kernel,
        out_shape=(
            jax.ShapeDtypeStruct((length, width), BF16),
            jax.ShapeDtypeStruct((NX * CAP, d), BF16),
            jax.ShapeDtypeStruct((NX, 2, ROWS), jnp.int32),
        ),
        in_specs=[vmem] * 7,
        out_specs=(vmem, vmem, vmem),
        scratch_shapes=[
            pltpu.VMEM((heads, 1, 128), F32),
            pltpu.VMEM((SEQ, 1, 128), F32),
            pltpu.VMEM((SEQ, 32, 128), BF16),
            pltpu.VMEM((SEQ, 32, 128), BF16),
            pltpu.VMEM((SEQ, 32, 128), BF16),
            pltpu.VMEM((SEQ, 32, 128), BF16),
            pltpu.VMEM((length, width), F32),
            pltpu.VMEM((length, width), F32),
            pltpu.VMEM((NX, CAP, d), BF16),
            pltpu.VMEM((NX, CAP, d), BF16),
            pltpu.VMEM((NX, 2, ROWS), jnp.int32),
            pltpu.SemaphoreType.DMA((8,)),
            pltpu.SemaphoreType.DMA((2,)),
        ],
        compiler_params=pltpu.CompilerParams(collective_id=0, has_side_effects=True),
        name="mamba",
    )(decay, x, b, c, skip_row, residual, ids_rows)


SPLIT = 1664
P_PART = (0, 768, SPLIT)
Q_PART = (SPLIT, SPLIT + 1152, 4096)
HALF = NZ // 2


def expert_kernel(
    mixed_ref, picked_ref, ids_rows_ref, ids_ref, residual_ref, gain_ref, router_ref,
    gate_hbm, up_hbm, down_hbm,
    out_ref,
    gate_w, up_w, down_w, m_send, g_in, t_in, held, part, hidden, gated, lifted,
    pz_in, py_in, qy_in, qz_in, ret_send, ret_in, stream, gate_col, stream16, result,
    load_sems, send_sems, recv_sems,
):
    me = lax.axis_index("seq")
    mx = lax.axis_index("exp")
    z = me // NY
    y = me % NY
    d_model = residual_ref.shape[1]
    d_part = d_model // NX

    loads = [
        pltpu.make_async_copy(src.at[0], dst, load_sems.at[i])
        for i, (src, dst) in enumerate(((gate_hbm, gate_w), (up_hbm, up_w), (down_hbm, down_w)))
    ]
    for load in loads:
        load.start()

    ahead_z = {"seq": (z + 1) % NZ * NY + y}
    behind_z = {"seq": (z + NZ - 1) % NZ * NY + y}
    ahead_y = {"seq": z * NY + (y + 1) % NY}
    behind_y = {"seq": z * NY + (y + NY - 1) % NY}
    to_z = {1: ahead_z, -1: behind_z}
    to_y = {1: ahead_y, -1: behind_y}

    barrier = pltpu.get_barrier_semaphore()
    for neighbour in (ahead_z, behind_z, ahead_y, behind_y):
        pl.semaphore_signal(barrier, inc=1, device_id=neighbour, device_id_type=MESH)
    for d in range(1, NX):
        pl.semaphore_signal(barrier, inc=1, device_id={"exp": (mx + d) % NX}, device_id_type=MESH)

    copies = {}

    def send(key, src, dst, device):
        i = len(copies)
        copy = pltpu.make_async_remote_copy(
            src_ref=src, dst_ref=dst, send_sem=send_sems.at[i], recv_sem=recv_sems.at[i],
            device_id=device, device_id_type=MESH,
        )
        copies[key] = copy
        copy.start()

    def arrived(key):
        copies[key].wait_recv()

    offset = jnp.zeros((NX * RUN_CAP, 1), F32)
    slot = (iota((NX * RUN_CAP, ROWS), 0) % RUN_CAP).astype(F32)
    rows = jnp.zeros((NX * RUN_CAP, d_part), F32)
    pack_slot = iota((RUN_CAP, NX * CAP), 0)
    pack_block = iota((RUN_CAP, NX * CAP), 1) // CAP
    pack_place = iota((RUN_CAP, NX * CAP), 1) % CAP
    back_slot = iota((NX * CAP, RUN_CAP), 1)
    back_block = iota((NX * CAP, RUN_CAP), 0) // CAP
    back_place = iota((NX * CAP, RUN_CAP), 0) % CAP
    pack = jnp.zeros((RUN_CAP, NX * CAP), F32)
    back = jnp.zeros((NX * CAP, RUN_CAP), F32)
    mine = jnp.zeros((1, 1), F32)
    for b in range(NX):
        first_row = ids_rows_ref[b][0:1, :]
        member, rank, count = block_select(first_row, NX, RUN_CAP)
        select = jnp.where(rank + offset == slot, member, 0.0).astype(BF16)
        rows += jnp.dot(select, mixed_ref[ROWS * b : ROWS * b + ROWS, :], preferred_element_type=F32)
        offset += count
        here = jnp.sum((first_row == mx).astype(F32), axis=1, keepdims=True)

        def match(of_block, of_place, of_slot):
            place = of_place.astype(F32)
            hit = (of_block == b) & (place < here) & (place + mine == of_slot.astype(F32))
            return hit.astype(F32)

        pack += match(pack_block, pack_place, pack_slot)
        back += match(back_block, back_place, back_slot)
        mine += here
    m_send[...] = rows.astype(BF16).reshape(NX, RUN_CAP, d_part)

    pl.semaphore_wait(barrier, 4 + NX - 1)
    for d in range(1, NX):
        to = (mx + d) % NX
        send(("row", d), m_send.at[to], g_in.at[mx], {"exp": to})
    for d in range(1, NX):
        to = (mx + d) % NX
        start_row = pl.multiple_of(to * ROWS, ROWS)
        send(("token", d), mixed_ref.at[pl.ds(start_row, ROWS), :], t_in.at[mx], {"exp": to})
    g_in[mx] = m_send[mx]
    t_in[mx] = mixed_ref[pl.ds(pl.multiple_of(mx * ROWS, ROWS), ROWS), :]

    gain = gain_ref[...]
    same = (iota((ROWS, ROWS), 0) == iota((ROWS, ROWS), 1)).astype(BF16)
    ids_cols = lax.dot_general(
        same, ids_ref[...].astype(F32).astype(BF16), CONTRACT_COLS, preferred_element_type=F32
    )

    def normalize(wide):
        return (wide * lax.rsqrt(jnp.mean(wide * wide, axis=-1, keepdims=True) + 1e-06) * gain).astype(BF16)

    stream16[...] = jnp.dot(pack.astype(BF16), picked_ref[...], preferred_element_type=F32)
    for d in range(1, NX):
        arrived(("row", d))
    for i in range(NX):
        cols = slice(d_part * i, d_part * i + d_part)
        stream16[:, cols] = (stream16[:, cols] + g_in[i].astype(F32)).astype(BF16).astype(F32)
    held[z, y] = normalize(stream16[...])

    whole_p = pl.ds(P_PART[0], P_PART[2] - P_PART[0])
    whole_q = pl.ds(Q_PART[0], Q_PART[2] - Q_PART[0])
    p_cols = (pl.ds(P_PART[0], P_PART[1] - P_PART[0]), pl.ds(P_PART[1], P_PART[2] - P_PART[1]))
    q_cols = (pl.ds(Q_PART[0], Q_PART[1] - Q_PART[0]), pl.ds(Q_PART[1], Q_PART[2] - Q_PART[1]))

    def far(way):
        return 0 if way == 1 else 1

    def pieces(way, distance, last):
        if distance == last:
            return (far(way),)
        return (far(way), 1 - far(way))

    def at_z(shift):
        return (z + shift + NZ) % NZ

    def at_y(shift):
        return (y + shift + NY) % NY

    def planes_of(distance):
        if distance == 0:
            return (0,)
        if distance == HALF:
            return (HALF,)
        return (-distance, distance)

    def share(key, ref, device):
        send(key, ref, ref, device)

    def q_round_y(plane):
        for way in (1, -1):
            share(("qy", plane, 1, way), held.at[at_z(plane), y, :, whole_q], to_y[way])

    def q_relay_y(plane):
        for way in (1, -1):
            arrived(("qy", plane, 1, way))
            share(("qy", plane, 2, way), held.at[at_z(plane), at_y(-way), :, q_cols[far(way)]], to_y[way])

    for way in (1, -1):
        share(("py", 1, way), held.at[z, y, :, whole_p], to_y[way])
        for piece in pieces(way, 1, HALF):
            share(("qz", 1, way, piece), held.at[z, y, :, q_cols[piece]], to_z[way])
    q_round_y(0)
    for way in (1, -1):
        arrived(("py", 1, way))
        share(("py", 2, way), held.at[z, at_y(-way), :, p_cols[far(way)]], to_y[way])
    q_relay_y(0)
    for way in (1, -1):
        arrived(("py", 2, way))
    for way in (1, -1):
        for piece in pieces(way, 1, HALF):
            share(("pz", 1, way, piece), held.at[z, :, :, p_cols[piece]], to_z[way])

    def own_tokens():
        for d in range(1, NX):
            arrived(("token", d))
        for i in range(NX):
            cols = slice(d_part * i, d_part * i + d_part)
            stream[:, cols] = (residual_ref[:, cols].astype(F32) + t_in[i].astype(F32)).astype(BF16)
        normed = normalize(stream[...].astype(F32))
        logits = lax.dot_general(normed, router_ref[...], CONTRACT_COLS, preferred_element_type=F32)
        experts = iota(logits.shape, 1).astype(F32)
        picks = [
            jnp.sum(jnp.where(experts == ids_cols[:, j : j + 1], logits, 0.0), axis=-1, keepdims=True)
            for j in range(2)
        ]
        gate_col[...] = jnp.broadcast_to(jax.nn.sigmoid(picks[0] - picks[1]), gate_col.shape)

    step_k = 512

    def compute(planes):
        for plane in planes:
            for way in (1, -1):
                arrived(("qy", plane, 2, way))
        count = len(planes) * NY * RUN_CAP
        gated[:count] = jnp.zeros((count, gated.shape[1]), F32)
        lifted[:count] = jnp.zeros((count, lifted.shape[1]), F32)

        def up_step(k, carry):
            depth = pl.ds(pl.multiple_of(k * step_k, step_k), step_k)
            blocks = [held[at_z(plane), :, :, depth].reshape(NY * RUN_CAP, step_k) for plane in planes]
            tokens = blocks[0] if len(blocks) == 1 else jnp.concatenate(blocks, axis=0)
            gated[:count] += jnp.dot(tokens, gate_w[depth, :], preferred_element_type=F32)
            lifted[:count] += jnp.dot(tokens, up_w[depth, :], preferred_element_type=F32)
            return carry

        lax.fori_loop(0, d_model // step_k, up_step, 0)
        hidden[:count] = (jax.nn.silu(gated[:count]) * lifted[:count]).astype(BF16)

        def down_step(n, carry):
            cols = pl.ds(pl.multiple_of(n * step_k, step_k), step_k)
            sums = jnp.dot(hidden[:count], down_w[:, cols], preferred_element_type=F32).astype(BF16)
            for i, plane in enumerate(planes):
                rows_of = sums[i * NY * RUN_CAP : (i + 1) * NY * RUN_CAP]
                part[at_z(plane), :, :, cols] = rows_of.reshape(NY, RUN_CAP, step_k)
            return carry

        lax.fori_loop(0, d_model // step_k, down_step, 0)

    for distance in range(1, HALF + 1):
        for way in (1, -1):
            for piece in pieces(way, distance, HALF):
                arrived(("qz", distance, way, piece))
                if distance < HALF and piece in pieces(way, distance + 1, HALF):
                    share(
                        ("qz", distance + 1, way, piece),
                        held.at[at_z(-way * distance), y, :, q_cols[piece]], to_z[way],
                    )
        for plane in planes_of(distance):
            q_round_y(plane)
        for way in (1, -1):
            for piece in pieces(way, distance, HALF):
                arrived(("pz", distance, way, piece))
                if distance < HALF and piece in pieces(way, distance + 1, HALF):
                    share(
                        ("pz", distance + 1, way, piece),
                        held.at[at_z(-way * distance), :, :, p_cols[piece]], to_z[way],
                    )
        for plane in planes_of(distance):
            q_relay_y(plane)
        if distance == 1:
            own_tokens()
            for load in loads:
                load.wait()
        compute(planes_of(distance - 1))

    def add(where, piece_in):
        total = part[where].astype(F32) + piece_in.astype(F32)
        part[where] = total.astype(BF16)

    def q_sum_start(plane):
        for way in (1, -1):
            cols = q_cols[far(way)]
            send(
                ("rqy", plane, 2, way), part.at[at_z(plane), at_y(2 * way), :, cols],
                qy_in.at[plane + HALF - 1, far(way), 1, :, pl.ds(cols.start - SPLIT, cols.size)], to_y[way],
            )

    def q_sum_relay(plane):
        for way in (1, -1):
            cols = q_cols[far(way)]
            arrived(("rqy", plane, 2, way))
            add(
                (at_z(plane), at_y(way), slice(None), cols),
                qy_in[plane + HALF - 1, far(way), 1, :, pl.ds(cols.start - SPLIT, cols.size)],
            )
            send(
                ("rqy", plane, 1, way), part.at[at_z(plane), at_y(way), :, whole_q],
                qy_in.at[plane + HALF - 1, far(way), 0], to_y[way],
            )

    def q_sum_y(plane):
        for way in (1, -1):
            arrived(("rqy", plane, 1, way))
        total = part[at_z(plane), y, :, whole_q].astype(F32)
        total += qy_in[plane + HALF - 1, 0, 0].astype(F32) + qy_in[plane + HALF - 1, 1, 0].astype(F32)
        return total

    def p_send(distance):
        for way in (1, -1):
            for piece in pieces(way, distance, HALF):
                cols = p_cols[piece]
                if distance < HALF and piece in pieces(way, distance + 1, HALF):
                    arrived(("rpz", distance + 1, way, piece))
                    add((at_z(way * distance), slice(None), slice(None), cols), pz_in[far(way), distance, :, :, cols])
                send(
                    ("rpz", distance, way, piece), part.at[at_z(way * distance), :, :, cols],
                    pz_in.at[far(way), distance - 1, :, :, cols], to_z[way],
                )

    def q_send(distance):
        for plane in planes_of(distance):
            part[at_z(plane), y, :, whole_q] = q_sum_y(plane).astype(BF16)
        for way in (1, -1):
            for piece in pieces(way, distance, HALF):
                cols = q_cols[piece]
                inner = pl.ds(cols.start - SPLIT, cols.size)
                if distance < HALF and piece in pieces(way, distance + 1, HALF):
                    arrived(("rqz", distance + 1, way, piece))
                    add((at_z(way * distance), y, slice(None), cols), qz_in[far(way), distance, :, inner])
                send(
                    ("rqz", distance, way, piece), part.at[at_z(way * distance), y, :, cols],
                    qz_in.at[far(way), distance - 1, :, inner], to_z[way],
                )

    for distance in range(HALF - 1, -1, -1):
        for plane in planes_of(distance):
            q_sum_start(plane)
    compute(planes_of(HALF))
    for plane in planes_of(HALF):
        q_sum_start(plane)
    p_send(HALF)
    for distance in range(HALF, -1, -1):
        for plane in planes_of(distance):
            q_sum_relay(plane)
    q_send(HALF)
    for distance in range(HALF - 1, 0, -1):
        p_send(distance)
        q_send(distance)

    for way in (1, -1):
        for piece in pieces(way, 1, HALF):
            arrived(("rpz", 1, way, piece))
    sums = part[z, :, :, whole_p].astype(F32) + pz_in[0, 0].astype(F32) + pz_in[1, 0].astype(F32)
    part[z, :, :, whole_p] = sums.astype(BF16)
    for way in (1, -1):
        cols = p_cols[far(way)]
        send(("rpy", 2, way), part.at[z, at_y(2 * way), :, cols], py_in.at[far(way), 1, :, cols], to_y[way])

    def give_back(cols, name):
        give = jnp.dot(back.astype(BF16), result[:, cols], preferred_element_type=F32)
        ret_send[:, :, cols] = give.astype(BF16).reshape(NX, CAP, cols.size)
        for d in range(1, NX):
            to = (mx + d) % NX
            send((name, d), ret_send.at[to, :, cols], ret_in.at[mx, :, cols], {"exp": to})
        ret_in[mx, :, cols] = ret_send[mx, :, cols]

    total = q_sum_y(0)
    for way in (1, -1):
        arrived(("rpy", 2, way))
        cols = p_cols[far(way)]
        add((z, at_y(way), slice(None), cols), py_in[far(way), 1, :, cols])
        send(("rpy", 1, way), part.at[z, at_y(way), :, whole_p], py_in.at[far(way), 0], to_y[way])
    for way in (1, -1):
        for piece in pieces(way, 1, HALF):
            arrived(("rqz", 1, way, piece))
    total += qz_in[0, 0].astype(F32) + qz_in[1, 0].astype(F32)
    result[:, whole_q] = total.astype(BF16)
    give_back(whole_q, "back_q")
    for way in (1, -1):
        arrived(("rpy", 1, way))
    total = part[z, y, :, whole_p].astype(F32) + py_in[0, 0].astype(F32) + py_in[1, 0].astype(F32)
    result[:, whole_p] = total.astype(BF16)
    give_back(whole_p, "back_p")

    own_expert = iota((ROWS, NX * CAP), 1) // CAP
    own_slot = iota((ROWS, NX * CAP), 1) % CAP
    member = (ids_cols[:, 0:1] == own_expert.astype(F32)).astype(F32)
    before = (iota((ROWS, ROWS), 1) < iota((ROWS, ROWS), 0)).astype(BF16)
    rank = jnp.dot(before, member.astype(BF16), preferred_element_type=F32)
    select = jnp.where(rank == own_slot.astype(F32), member, 0.0).astype(BF16)
    for name, cols in (("back_q", whole_q), ("back_p", whole_p)):
        for d in range(1, NX):
            arrived((name, d))
        combined = jnp.dot(select, ret_in[:, :, cols].reshape(NX * CAP, cols.size), preferred_element_type=F32)
        out_ref[:, cols] = (stream[:, cols].astype(F32) + gate_col[:, 0:1] * combined).astype(BF16)
    for copy in copies.values():
        copy.wait_send()


def experts(mixed, picked, ids_rows, ids, residual, gain, router, gate_weight, up_weight, down_weight):
    rows, d = residual.shape
    units = gate_weight.shape[2]
    d_part = mixed.shape[1]
    vmem = pl.BlockSpec(memory_space=pltpu.VMEM)
    hbm = pl.BlockSpec(memory_space=pl.ANY)
    p_width, q_width = SPLIT, d - SPLIT
    return pl.pallas_call(
        expert_kernel,
        out_shape=jax.ShapeDtypeStruct((rows, d), BF16),
        in_specs=[vmem] * 7 + [hbm] * 3,
        out_specs=vmem,
        scratch_shapes=[
            pltpu.VMEM((d, units), BF16),
            pltpu.VMEM((d, units), BF16),
            pltpu.VMEM((units, d), BF16),
            pltpu.VMEM((NX, RUN_CAP, d_part), BF16),
            pltpu.VMEM((NX, RUN_CAP, d_part), BF16),
            pltpu.VMEM((NX, ROWS, d_part), BF16),
            pltpu.VMEM((NZ, NY, RUN_CAP, d), BF16),
            pltpu.VMEM((NZ, NY, RUN_CAP, d), BF16),
            pltpu.VMEM((2 * NY * RUN_CAP, units), BF16),
            pltpu.VMEM((2 * NY * RUN_CAP, units), F32),
            pltpu.VMEM((2 * NY * RUN_CAP, units), F32),
            pltpu.VMEM((2, HALF, NY, RUN_CAP, p_width), BF16),
            pltpu.VMEM((2, 2, RUN_CAP, p_width), BF16),
            pltpu.VMEM((NZ, 2, 2, RUN_CAP, q_width), BF16),
            pltpu.VMEM((2, HALF, RUN_CAP, q_width), BF16),
            pltpu.VMEM((NX, CAP, d), BF16),
            pltpu.VMEM((NX, CAP, d), BF16),
            pltpu.VMEM((rows, d), BF16),
            pltpu.VMEM((rows, 128), F32),
            pltpu.VMEM((RUN_CAP, d), F32),
            pltpu.VMEM((RUN_CAP, d), BF16),
            pltpu.SemaphoreType.DMA((3,)),
            pltpu.SemaphoreType.DMA((160,)),
            pltpu.SemaphoreType.DMA((160,)),
        ],
        compiler_params=pltpu.CompilerParams(
            collective_id=1, has_side_effects=True, vmem_limit_bytes=60 * 1024 * 1024
        ),
        name="experts",
    )(mixed, picked, ids_rows, ids, residual, gain, router, gate_weight, up_weight, down_weight)


def body(
    head_inputs, input_matrix, output_matrix, log_decay, skip_gain, residual, norm_gain,
    router_weight, expert_ids, gate_weight, up_weight, down_weight,
):
    ids = expert_ids.T
    mixed, picked, ids_all = mamba(
        head_inputs, input_matrix, output_matrix, log_decay, skip_gain[None, :], residual, ids
    )
    return experts(
        mixed, picked, ids_all, ids, residual, norm_gain[None, :], router_weight.T,
        gate_weight, up_weight, down_weight,
    )


def solution(mesh):
    return jax.shard_map(
        body,
        mesh=mesh,
        in_specs=(
            P(("dp", "seq"), "exp"),
            P(("dp", "seq"), None),
            P(("dp", "seq"), None),
            P("exp", ("dp", "seq")),
            P("exp"),
            P(("dp", "seq", "exp"), None),
            P(),
            P(),
            P(("dp", "seq", "exp"), None),
            P("exp", None, "seq"),
            P("exp", None, "seq"),
            P("exp", "seq", None),
        ),
        out_specs=P(("dp", "seq", "exp"), None),
        check_vma=False,
    )
```
